32 devices in a mesh: energy: 16 (over z, y, core), section: 2 (over x).
Axes of the slice: x: 2, y: 2, z: 4, core: 2. Of those that a mesh axis runs over, the one named last changes fastest.
Arguments:
- green_free: bfloat16 [64, 2, 2, 384, 384], P('energy', 'section'), may hold values from -1 to 1
- lesser_source: bfloat16 [64, 2, 2, 384, 384], P('energy', 'section'), may hold values from -1 to 1
- coupling: bfloat16 [2, 384, 384], P('section'), may hold values from -0.21875 to 0.21875
- scatter_strength: bfloat16 [384, 384], replicated, may hold values from 0.19921875 to 1
- counts: int32 [16], replicated, may hold values from 1 to 4, as said below
Outputs:
- green_diag: bfloat16 [64, 2, 2, 384, 384], P('energy', 'section')
- lesser_diag: bfloat16 [64, 2, 2, 384, 384], P('energy', 'section')
- sigma_green: bfloat16 [64, 2, 2, 384, 384], P('energy', 'section')
- sigma_lesser: bfloat16 [64, 2, 2, 384, 384], P('energy', 'section')
The draws below stay inside these ranges and needn't reach their ends.
Inputs may be any that keep to these rules, and one draw needn't show every extreme that they name: `counts`: at least one window has 4 live points.
All inputs are finite; a program needn't handle non-finite values.
Results may differ from the reference program's by a relative error of at most 0.013.
Values may be sent and summed in bfloat16 or wider, within the bound.
No kernel may reach another device: no remote copies, remote signals or barrier semaphores. Data moves between devices by JAX's collectives and lax.ppermute only.
A program may use at most 128 MiB of HBM per device.

```python
import math
import jax
import jax.numpy as jnp
from jax import lax

M = 384
SLOTS = 4
WINDOWS = 16
ENERGIES = 64
LAYERS = 2


def layered_blocks(key, diag_lo, diag_hi, imag_lo, imag_hi):
    key_noise, key_real, key_imag = jax.random.split(key, 3)
    spread = 0.3
    noise = jax.random.normal(key_noise, (ENERGIES, LAYERS, 2, M, M), jnp.float32) * (spread / math.sqrt(M))
    real_diag = jax.random.uniform(key_real, (ENERGIES, LAYERS, M), jnp.float32, diag_lo, diag_hi)
    imag_diag = jax.random.uniform(key_imag, (ENERGIES, LAYERS, M), jnp.float32, imag_lo, imag_hi)
    identity = jnp.eye(M, dtype=jnp.float32)
    diagonal = jnp.stack((real_diag, imag_diag), axis=2)[..., :, None] * identity
    return (diagonal + noise).astype(jnp.bfloat16)


def draw_green_free(key, part):
    return layered_blocks(jax.random.fold_in(key, 11), 0.3, 0.7, -0.4, -0.1)


def draw_lesser_source(key, part):
    return layered_blocks(jax.random.fold_in(key, 23), -0.2, 0.2, 0.1, 0.5)


def draw_counts(key, part):
    key_counts, key_full = jax.random.split(jax.random.fold_in(key, 37))
    values = jax.random.randint(key_counts, (WINDOWS,), 1, SLOTS + 1, jnp.int32)
    chosen = jax.random.randint(key_full, (), 0, WINDOWS, jnp.int32)
    return jnp.where(jnp.arange(WINDOWS, dtype=jnp.int32) == chosen, SLOTS, values).astype(jnp.int32)


def levels(key, shape, cuts, low, largest):
    factor_of, own = 1.0, jax.random.fold_in(key, 6)
    for position, blocks in cuts:
        draws = jnp.exp(jax.random.uniform(jax.random.fold_in(own, position), (blocks,), jnp.float32, low / len(cuts), largest / len(cuts)))
        factor_of = factor_of * jnp.repeat(draws, shape[position] // blocks).reshape([-1 if axis == position else 1 for axis in range(len(shape))])
    return factor_of


def bell_draw(rng, shape, scale, bound, shards=(), kind=jnp.bfloat16):
    entries = jax.random.normal(rng, shape, jnp.float32) * scale
    if len(shards) > 0:
        entries = levels(rng, shape, shards, -0.22, 0.18) * entries
    return jnp.clip(entries, min=-bound, max=bound).astype(kind)


def setup_inputs(seed: int = 0) -> dict:
    key_of = jax.random.split(jax.random.key(seed), 6)
    return {
        "green_free": draw_green_free(jax.random.fold_in(key_of[5], 71), 0),
        "lesser_source": draw_lesser_source(jax.random.fold_in(key_of[5], 71), 0),
        "coupling": bell_draw(key_of[2], (LAYERS, M, M), (2 * M) ** -0.5, 0.21875, ((0, 2),)),
        "scatter_strength": jnp.clip(jax.random.uniform(key_of[3], (M, M), jnp.float32, 0.19921875, 1.0), 0.19921875, 1.0).astype(jnp.bfloat16),
        "counts": draw_counts(jax.random.fold_in(key_of[5], 71), 0),
    }


def matmul(left, right):
    return jnp.dot(left, right, preferred_element_type=jnp.float32)


def complex_product(left, right):
    real_part = matmul(left[0], right[0]) - matmul(left[1], right[1])
    imag_part = matmul(left[0], right[1]) + matmul(left[1], right[0])
    return jnp.stack((real_part, imag_part))


def adjoint_product(left, right):
    real_part = matmul(left[0], right[0].T) + matmul(left[1], right[1].T)
    imag_part = matmul(left[1], right[0].T) - matmul(left[0], right[1].T)
    return jnp.stack((real_part, imag_part))


def real_right(left, hopping):
    return jnp.stack((matmul(left[0], hopping), matmul(left[1], hopping)))


def real_left(hopping, right):
    return jnp.stack((matmul(hopping, right[0]), matmul(hopping, right[1])))


def forward_layer(green_prev, lesser_prev, bare, source, hopping):
    low = jnp.bfloat16
    carried = real_right(green_prev, hopping).astype(low)
    coupled = real_left(hopping.T, carried).astype(low)
    dressed = complex_product(bare, coupled).astype(low)
    green = (bare.astype(jnp.float32) + complex_product(dressed, bare)).astype(low)
    carried_l = real_right(lesser_prev, hopping).astype(low)
    kernel = (source.astype(jnp.float32) + real_left(hopping.T, carried_l)).astype(low)
    half_l = complex_product(green, kernel).astype(low)
    lesser = adjoint_product(half_l, green).astype(low)
    return green, lesser


def backward_layer(block_in, blockl_in, green, lesser, hopping):
    low = jnp.bfloat16
    dressed = complex_product(green, block_in).astype(low)
    full_green = (green.astype(jnp.float32) + complex_product(dressed, green)).astype(low)
    dressed_l = complex_product(green, blockl_in).astype(low)
    full_lesser = (lesser.astype(jnp.float32) + adjoint_product(dressed_l, green)).astype(low)
    half = real_right(full_green, hopping.T).astype(low)
    block_out = real_left(hopping, half).astype(low)
    half_l = real_right(full_lesser, hopping.T).astype(low)
    blockl_out = real_left(hopping, half_l).astype(low)
    return full_green, full_lesser, block_out, blockl_out


def reference(green_free, lesser_source, coupling, scatter_strength, counts):
    energy_ids = jnp.arange(ENERGIES, dtype=jnp.int32)
    window_ids = (energy_ids // SLOTS).astype(jnp.int32)
    live = (energy_ids % SLOTS) < counts[window_ids]

    def one_energy(inputs):
        bare_all, source_all, is_live = inputs
        empty = jnp.zeros((2, M, M), bare_all.dtype)

        def forward_step(carry, pieces):
            green, lesser = forward_layer(carry[0], carry[1], pieces[0], pieces[1], pieces[2])
            return (green, lesser), (green, lesser)

        _, (greens, lessers) = lax.scan(forward_step, (empty, empty), (bare_all, source_all, coupling))

        def backward_step(carry, pieces):
            full_green, full_lesser, block_out, blockl_out = backward_layer(carry[0], carry[1], pieces[0], pieces[1], pieces[2])
            return (block_out, blockl_out), (full_green, full_lesser)

        _, (full_g, full_l) = lax.scan(backward_step, (empty, empty), (greens, lessers, coupling), reverse=True)
        full_g = jnp.where(is_live, full_g, jnp.zeros_like(full_g))
        full_l = jnp.where(is_live, full_l, jnp.zeros_like(full_l))
        return full_g, full_l

    green_diag, lesser_diag = lax.map(one_energy, (green_free, lesser_source, live))
    padding = jnp.zeros((SLOTS,) + green_diag.shape[1:], green_diag.dtype)
    strength = scatter_strength.astype(jnp.float32)

    def update(blocks):
        extended = jnp.concatenate([padding, blocks, padding], axis=0)
        below = extended[:ENERGIES]
        above = extended[2 * SLOTS:]
        return (strength * (below.astype(jnp.float32) + above.astype(jnp.float32))).astype(jnp.bfloat16)

    return green_diag, lesser_diag, update(green_diag), update(lesser_diag)
```

```python
import functools

import jax
import jax.numpy as jnp
from jax import lax
from jax.experimental import pallas as pl
from jax.experimental.pallas import tpu as pltpu
from jax.sharding import PartitionSpec as P


LOW = jnp.bfloat16
FULL = jnp.float32


def dot(left, right):
    return jnp.dot(left, right, preferred_element_type=FULL)


def dot_flip(left, right):
    return lax.dot_general(left, right, (((1,), (1,)), ((), ())), preferred_element_type=FULL)


def real_form(form, block):
    size = block.shape[0]
    real, imag = block[:, :size], block[:, size:]
    form[:size, :size] = real
    form[:size, size:] = imag
    form[size:, :size] = -imag
    form[size:, size:] = real


def sandwich(first, block, second):
    size = block.shape[0]
    half = jnp.concatenate(
        (dot(block[:, :size], second), dot(block[:, size:], second)), axis=1
    ).astype(LOW)
    return dot(first, half)


def wide(pair):
    return jnp.concatenate((pair[0], pair[1]), axis=1)


def store_pair(refs, block):
    size = block.shape[0]
    for ref in refs:
        ref[0] = block[:, :size]
        ref[1] = block[:, size:]


def pick(flags, own, other, low_ref, high_ref):
    @pl.when(flags[0] == 0)
    def _():
        low_ref[...] = wide(own)
        high_ref[...] = wide(other)

    @pl.when(flags[0] != 0)
    def _():
        low_ref[...] = wide(other)
        high_ref[...] = wide(own)


def green_kernel(slot, flags, own, other, hop, hop_t, *rest):
    piece, upper, full, low, high, form = rest[-6:]

    @pl.when(slot < flags[1])
    def _():
        pick(flags, own[0, 0], other, low, high)
        coupled = sandwich(hop_t[...], low[...], hop[...]).astype(LOW)
        real_form(form, coupled)
        dressed = dot(high[...], form[...]).astype(LOW)
        real_form(form, high[...])
        green = (high[...].astype(FULL) + dot(dressed, form[...])).astype(LOW)
        store_pair((upper,), green)

        @pl.when(flags[0] != 0)
        def _():
            store_pair((piece, full.at[0, 0]), green)

        @pl.when(flags[0] == 0)
        def _():
            high[...] = green
            block = sandwich(hop[...], high[...], hop_t[...]).astype(LOW)
            real_form(form, block)
            dressed = dot(low[...], form[...]).astype(LOW)
            real_form(form, low[...])
            whole = (low[...].astype(FULL) + dot(dressed, form[...])).astype(LOW)
            store_pair((piece, full.at[0, 0]), whole)

    @pl.when(slot >= flags[1])
    def _():
        piece[...] = jnp.zeros_like(piece)
        upper[...] = jnp.zeros_like(upper)
        full[...] = jnp.zeros_like(full)


def lesser_kernel(slot, flags, own_g, other_g, upper, own, other, hop, hop_t, *rest):
    piece, full, low, high, form, low_form, high_form, lower, source = rest[-9:]

    @pl.when(slot < flags[1])
    def _():
        @pl.when(flags[0] == 0)
        def _():
            low[...] = wide(own_g[0, 0])

        @pl.when(flags[0] != 0)
        def _():
            low[...] = wide(other_g)

        pick(flags, own[0, 0], other, lower, source)
        real_form(low_form, low[...])
        real_form(form, lower[...])
        half = dot(low[...], form[...]).astype(LOW)
        lower[...] = dot_flip(half, low_form[...]).astype(LOW)
        high[...] = wide(upper)
        real_form(high_form, high[...])
        kernel = (source[...].astype(FULL) + sandwich(hop_t[...], lower[...], hop[...])).astype(LOW)
        real_form(form, kernel)
        half = dot(high[...], form[...]).astype(LOW)
        lesser = dot_flip(half, high_form[...]).astype(LOW)

        @pl.when(flags[0] != 0)
        def _():
            store_pair((piece, full.at[0, 0]), lesser)

        @pl.when(flags[0] == 0)
        def _():
            source[...] = lesser
            block = sandwich(hop[...], source[...], hop_t[...]).astype(LOW)
            real_form(form, block)
            dressed = dot(low[...], form[...]).astype(LOW)
            whole = (lower[...].astype(FULL) + dot_flip(dressed, low_form[...])).astype(LOW)
            store_pair((piece, full.at[0, 0]), whole)

    @pl.when(slot >= flags[1])
    def _():
        piece[...] = jnp.zeros_like(piece)
        full[...] = jnp.zeros_like(full)


def sigma_kernel(slot, first, second, strength, *rest):
    full = rest[-1]
    total = first[...].astype(FULL) + second[...].astype(FULL)
    full[0, 0] = (strength[...].astype(FULL) * total).astype(LOW)


def whole_spec(array):
    zeros = (0,) * array.ndim
    return pl.BlockSpec(array.shape, lambda i, *_: zeros)


def slot_spec(slot, array):
    return pl.BlockSpec((1,) + array.shape[1:], lambda i, *_: (slot, 0, 0, 0, 0))


def run(body, name, slot, flags, ins, full_shape, full, pieces, scratch, flops):
    specs = [slot_spec(slot, a) if a.ndim == 5 else whole_spec(a) for a in ins]
    args = list(ins)
    prefetch = [] if flags is None else [flags]
    aliases = {}
    if full is not None:
        specs.append(pl.BlockSpec(memory_space=pl.ANY))
        aliases = {len(prefetch) + len(args): len(pieces)}
        args.append(full)
    full_struct = jax.ShapeDtypeStruct(full_shape, LOW)
    out_shape = tuple(pieces) + (full_struct,)
    out_specs = tuple(whole_spec(p) for p in pieces) + (slot_spec(slot, full_struct),)
    bytes_moved = sum(2 * p.size for p in pieces) * 4
    return pl.pallas_call(
        functools.partial(body, slot),
        out_shape=out_shape,
        grid_spec=pltpu.PrefetchScalarGridSpec(
            num_scalar_prefetch=len(prefetch),
            grid=(1,),
            in_specs=specs,
            out_specs=out_specs,
            scratch_shapes=scratch,
        ),
        input_output_aliases=aliases,
        cost_estimate=pl.CostEstimate(flops=flops, bytes_accessed=bytes_moved, transcendentals=0),
        name=name,
    )(*prefetch, *args)


def swap_pairs(count, start):
    pairs = []
    for i in range(start, count - 1, 2):
        pairs += [(i, i + 1), (i + 1, i)]
    return pairs


def on_device(green_free, lesser_source, coupling, scatter_strength, counts):
    slots = green_free.shape[0]
    size = green_free.shape[-1]
    sections = lax.axis_size("section")
    windows = lax.axis_size("energy")
    assert sections == 2 and green_free.shape[1] == 1
    section = lax.axis_index("section")
    window = lax.axis_index("energy")
    flags = jnp.stack((section.astype(jnp.int32), counts[window]))

    def across(array):
        return lax.ppermute(array, "section", [(0, 1), (1, 0)])

    def inner(array):
        return lax.ppermute(array, "energy", swap_pairs(windows, 0))

    def outer(array):
        return lax.ppermute(array, "energy", swap_pairs(windows, 1))

    own_hop = coupling[0]
    other_hop = lax.ppermute(own_hop, "section", [(1, 0)])
    hop = jnp.where(section == 1, own_hop, other_hop)
    hop_t = hop.T

    moved = []
    for slot in range(slots):
        moved.append((across(green_free[slot, 0]), across(lesser_source[slot, 0])))

    pair = jax.ShapeDtypeStruct((2, size, size), LOW)
    wide_block = pltpu.VMEM((size, 2 * size), LOW)
    form_block = pltpu.VMEM((2 * size, 2 * size), LOW)
    unit = 2 * size**3
    green_diag = lesser_diag = sigma_green = sigma_lesser = None
    shape = green_free.shape
    for slot in range(slots):
        other_g, other_l = moved[slot]
        piece_g, upper, green_diag = run(
            green_kernel,
            "green_block",
            slot,
            flags,
            [green_free, other_g, hop, hop_t],
            shape,
            green_diag,
            [pair, pair],
            [wide_block, wide_block, form_block],
            24 * unit,
        )
        first, second = inner(piece_g), outer(piece_g)
        (sigma_green,) = run(
            sigma_kernel, "sigma_green_block", slot, None, [first, second, scatter_strength], shape, sigma_green, [], [], unit // 100
        )
        piece_l, lesser_diag = run(
            lesser_kernel,
            "lesser_block",
            slot,
            flags,
            [green_free, other_g, upper, lesser_source, other_l, hop, hop_t],
            shape,
            lesser_diag,
            [pair],
            [wide_block, wide_block, form_block, form_block, form_block, wide_block, wide_block],
            32 * unit,
        )
        first, second = inner(piece_l), outer(piece_l)
        (sigma_lesser,) = run(
            sigma_kernel, "sigma_lesser_block", slot, None, [first, second, scatter_strength], shape, sigma_lesser, [], [], unit // 100
        )
    return (green_diag, lesser_diag, sigma_green, sigma_lesser)


def solution(mesh):
    placed = (
        P("energy", "section", None, None, None),
        P("energy", "section", None, None, None),
        P("section", None, None),
        P(),
        P(),
    )
    return jax.shard_map(
        on_device,
        mesh=mesh,
        in_specs=placed,
        out_specs=(P("energy", "section", None, None, None),) * 4,
        check_vma=False,
    )
```
